256 devices in a mesh: ex: 8 (over z_hi, x), hid: 32 (over y, z_lo, core).
Axes of the slice: x: 4, y: 4, z: 8 (z_hi: 2, z_lo: 4; z = z_hi * 4 + z_lo), core: 2. Of those that a mesh axis runs over, the one named last changes fastest.
Arguments:
- activations: float32 [16384, 28672], P('ex', 'hid'), may hold values from -6 to 6
- out_grads: float32 [16384, 8192], P('ex', 'hid'), may hold values from -6 to 6
- input_proj: float32 [28672, 64], P('hid'), may hold values from -0.03125 to 0.03125
- output_proj: float32 [8192, 64], P('hid'), may hold values from -0.0625 to 0.0625
- query_grads: float32 [4096, 4096], P('ex', 'hid'), may hold values from -0.00390625 to 0.00390625
Outputs:
- scores: float32 [32, 4096], P('ex', 'hid')
The draws below stay inside these ranges and needn't reach their ends.
All inputs are finite; a program needn't handle non-finite values.
Results may differ from the reference program's by a relative error of at most 0.00017.
Values sent between devices are 32-bit elements; how exact they have to be, the bound alone decides.
No kernel may reach another device: no remote copies, remote signals or barrier semaphores. Data moves between devices by JAX's collectives and lax.ppermute only.
A program may use at most 64 MiB of HBM per device.

```python
import jax
import jax.numpy as jnp
from jax import lax

D_IN = 28672
D_OUT = 8192
RANK = 64
SEQ = 512
FEAT = 4096
ROWS = 16384
QUERIES = 4096


def block_scale(rng, dims, split, low, high):
    def one(dim, parts):
        draws = jax.random.uniform(jax.random.fold_in(jax.random.fold_in(rng, 6), dim), (parts,), jnp.float32, low / len(split), high / len(split))
        return jnp.repeat(jnp.exp(draws), dims[dim] // parts).reshape((-1,) + (1,) * (len(dims) - dim - 1))

    factor_of = one(*split[0])
    for cut in split[1:]:
        factor_of = factor_of * one(*cut)
    return factor_of


def normal_values(rng, dims, width, reach, cuts=(), held_as=jnp.bfloat16):
    result = jax.random.normal(rng, dims, jnp.float32) * width
    if len(cuts) > 0:
        result = block_scale(rng, dims, cuts, -0.22, 0.18) * result
    return jnp.clip(result, min=-reach, max=reach).astype(held_as)


def setup_inputs(seed: int = 0) -> dict:
    arg_keys = jax.random.split(jax.random.key(seed), 6)
    activations = normal_values(arg_keys[0], (ROWS, D_IN), 1.0, 6.0, ((0, 8), (1, 32)), jnp.float32)
    out_grads = normal_values(arg_keys[1], (ROWS, D_OUT), 1.0, 6.0, ((0, 8), (1, 32)), jnp.float32)
    input_proj = normal_values(arg_keys[2], (D_IN, RANK), D_IN ** -0.5, 0.03125, ((0, 32),), jnp.float32)
    output_proj = normal_values(arg_keys[3], (D_OUT, RANK), D_OUT ** -0.5, 0.0625, ((0, 32),), jnp.float32)
    query_grads = normal_values(arg_keys[4], (FEAT, QUERIES), (FEAT * SEQ) ** -0.5, 0.00390625, ((0, 8), (1, 32)), jnp.float32)
    return {"activations": activations, "out_grads": out_grads, "input_proj": input_proj, "output_proj": output_proj, "query_grads": query_grads}


def reference(activations, out_grads, input_proj, output_proj, query_grads):
    highest = lax.Precision.HIGHEST
    inputs = activations.reshape(-1, SEQ, D_IN)
    errors = out_grads.reshape(-1, SEQ, D_OUT)

    def single(pair):
        x_rows, g_rows = pair
        in_low = jnp.dot(x_rows, input_proj, precision=highest, preferred_element_type=jnp.float32)
        out_low = jnp.dot(g_rows, output_proj, precision=highest, preferred_element_type=jnp.float32)
        return jnp.dot(out_low.T, in_low, precision=highest, preferred_element_type=jnp.float32).reshape(-1)

    grads = lax.map(single, (inputs, errors))
    return jnp.dot(grads, query_grads, precision=highest, preferred_element_type=jnp.float32)
```

```python
import functools

import jax
import jax.numpy as jnp
from jax import lax
from jax.experimental import pallas as pl
from jax.experimental.pallas import tpu as pltpu
from jax.sharding import Mesh, PartitionSpec as P

RANK = 64
SEQ = 512
E_DEV = 4
FEAT = 4096
LANES = 128
HALF = SEQ // 2
CHUNK = HALF // 4
HID = ("y", "zl", "c")
EX = ("zh", "x")
F32 = jnp.float32
BF16 = jnp.bfloat16


def split(value):
    high = value.astype(BF16)
    low = (value - high.astype(F32)).astype(BF16)
    return high, low


def project_kernel(pos_ref, x_ref, g_ref, px_ref, pa_ref, pb_ref, keep_ref, send_ref, wx_ref, wg_ref):
    step = pl.program_id(0)

    @pl.when(step == 0)
    def _():
        xh, xl = split(px_ref[...].T)
        zx = jnp.zeros_like(xh)
        wx_ref[...] = jnp.concatenate([zx, xh, zx, xl], axis=1)
        order = [pl.ds(parity, RANK // 2, stride=2) for parity in range(2)]
        halves = [jnp.concatenate([ref[rows, :] for rows in order], axis=0).T for ref in (pa_ref, pb_ref)]
        gh, gl = split(jnp.concatenate(halves, axis=0))
        zg = jnp.zeros_like(gh)
        wg_ref[...] = jnp.concatenate([gh, zg, gl, zg], axis=1)

    xh, xl = split(x_ref[...])
    gh, gl = split(g_ref[...])
    dot = functools.partial(jnp.dot, preferred_element_type=F32)
    acc = dot(xh, wx_ref[...]) + dot(xl, wx_ref[...]) + dot(gh, wg_ref[...]) + dot(gl, wg_ref[...])
    total = acc[:, :LANES] + acc[:, LANES:]

    def put(ref):
        for q in range(4):
            at = pl.multiple_of((q ^ pos_ref[1]) * CHUNK, CHUNK)
            ref[0, pl.ds(at, CHUNK), :] = total[q * CHUNK : (q + 1) * CHUNK]

    mine = (step % 2) == pos_ref[2]

    @pl.when(mine)
    def _():
        put(keep_ref)

    @pl.when(jnp.logical_not(mine))
    def _():
        put(send_ref)


def project(pos, activations, out_grads, input_proj, output_proj):
    d_in, d_out = activations.shape[1], out_grads.shape[1]
    out_spec = pl.BlockSpec((1, HALF, LANES), lambda i, pos: ((i // 2) ^ pos[0], 0, 0))
    shape = jax.ShapeDtypeStruct((E_DEV, HALF, LANES), F32)
    return pl.pallas_call(
        project_kernel,
        out_shape=(shape, shape),
        grid_spec=pltpu.PrefetchScalarGridSpec(
            num_scalar_prefetch=1,
            grid=(2 * E_DEV,),
            in_specs=[
                pl.BlockSpec((HALF, d_in), lambda i, pos: (i, 0)),
                pl.BlockSpec((HALF, d_out), lambda i, pos: (i, 0)),
                pl.BlockSpec((RANK, d_in), lambda i, pos: (0, 0)),
                pl.BlockSpec((RANK, LANES), lambda i, pos: (0, 0)),
                pl.BlockSpec((RANK, LANES), lambda i, pos: (0, 1)),
            ],
            out_specs=[out_spec, out_spec],
            scratch_shapes=[pltpu.VMEM((d_in, 2 * LANES), BF16), pltpu.VMEM((d_out, 2 * LANES), BF16)],
        ),
        compiler_params=pltpu.CompilerParams(vmem_limit_bytes=58 << 20),
        name="project",
    )(pos, activations, out_grads, input_proj.T, output_proj.T, output_proj.T)


def outer_kernel(a_ref, b_ref, c_ref, d_ref, out_ref):
    rows = a_ref[...] + b_ref[...] + c_ref[...] + d_ref[...]
    high, low = split(rows.T[:RANK])
    xh, xl = split(rows)
    dot = functools.partial(jnp.dot, preferred_element_type=F32)
    acc = dot(high, xh) + dot(high, xl) + dot(low, xh)
    right = acc[:, RANK:]
    out_ref[...] = jnp.concatenate([right[: RANK // 2], right[RANK // 2 :]], axis=1)


def outer(pieces):
    return pl.pallas_call(
        outer_kernel,
        out_shape=jax.ShapeDtypeStruct((FEAT // LANES, LANES), F32),
        compiler_params=pltpu.CompilerParams(vmem_limit_bytes=4 << 20),
        name="outer",
    )(*pieces)


def score_kernel(pos_ref, grads_ref, *refs):
    blocks, (out_ref, all_ref) = refs[:8], refs[8:]
    tiles = FEAT // LANES
    for e in range(E_DEV):
        all_ref[e * tiles : (e + 1) * tiles, :] = (
            grads_ref[4 * e] + grads_ref[4 * e + 1] + grads_ref[4 * e + 2] + grads_ref[4 * e + 3]
        )
    acc = jnp.zeros((2 * E_DEV, 2 * LANES), F32)
    for dz in range(2):
        for dx in range(4):
            base = ((pos_ref[3] ^ dz) * 4 + (pos_ref[4] ^ dx)) * 4
            left = jnp.concatenate(
                [all_ref[pl.ds(base + t, E_DEV, stride=tiles), :] for t in range(4)], axis=1
            )
            lh, ll = split(left)
            lhs = jnp.concatenate([lh.astype(F32), ll.astype(F32)], axis=0).astype(BF16)
            qh, ql = split(blocks[dz * 4 + dx][...])
            acc = acc + jnp.dot(lhs, jnp.concatenate([qh, ql], axis=1), preferred_element_type=F32)
    out_ref[...] = acc[:E_DEV, :LANES] + (acc[:E_DEV, LANES:] + acc[E_DEV:, :LANES])


def score(pos, grads, blocks):
    vmem = pl.BlockSpec(memory_space=pltpu.VMEM)
    return pl.pallas_call(
        score_kernel,
        out_shape=jax.ShapeDtypeStruct((E_DEV, LANES), F32),
        in_specs=[pl.BlockSpec(memory_space=pltpu.SMEM)] + [vmem] * 9,
        out_specs=vmem,
        scratch_shapes=[pltpu.VMEM((FEAT // LANES * E_DEV, LANES), F32)],
        compiler_params=pltpu.CompilerParams(vmem_limit_bytes=24 << 20),
        name="score",
    )(pos, grads, *blocks)


def swap(value, axis, size, bits):
    return lax.ppermute(value, axis, [(i, i ^ bits) for i in range(size)])


def on_device(activations, out_grads, input_proj, output_proj, query_grads):
    pos = jnp.stack([lax.axis_index(a) for a in ("y", "zl", "c", "zh", "x")]).astype(jnp.int32)
    far = swap(query_grads, "zh", 2, 1)
    blocks = [query_grads] + [swap(query_grads, "x", 4, k) for k in (1, 2, 3)]
    blocks += [far] + [swap(far, "x", 4, k) for k in (1, 2, 3)]

    keep, send = project(pos, activations, out_grads, input_proj, output_proj)
    part = keep + swap(send, "c", 2, 1)
    rows = part[0] + sum(swap(part[k], "y", 4, k) for k in (1, 2, 3))
    pieces = [rows[m * CHUNK : (m + 1) * CHUNK] for m in range(4)]
    pieces = pieces[:1] + [swap(pieces[m], "zl", 4, m) for m in (1, 2, 3)]
    grads = outer(pieces)
    grads = grads + swap(grads, "c", 2, 1)
    spread = jnp.broadcast_to(grads[None], (16,) + grads.shape)
    gathered = lax.all_to_all(spread, ("y", "zl"), 0, 0, tiled=True)
    return score(pos, gathered, blocks)


def solution(mesh):
    fine = Mesh(mesh.devices.reshape(2, 4, 4, 4, 2), EX + HID)
    placed = (P(EX, HID), P(EX, HID), P(HID, None), P(HID, None), P(EX, HID))
    return jax.shard_map(on_device, mesh=fine, in_specs=placed, out_specs=P(EX, HID), check_vma=False)
```

```python
import functools

import jax
import jax.numpy as jnp
from jax import lax
from jax.experimental import pallas as pl
from jax.experimental.pallas import tpu as pltpu
from jax.sharding import Mesh, PartitionSpec as P

RANK = 64
SEQ = 512
E_DEV = 4
FEAT = 4096
LANES = 128
HALF = SEQ // 2
CHUNK = HALF // 4
SIZES = (512, 512, 512, 512)
HID = ("y", "zl", "c")
EX = ("zh", "x")
F32 = jnp.float32
BF16 = jnp.bfloat16


def split(value):
    high = value.astype(BF16)
    low = (value - high.astype(F32)).astype(BF16)
    return high, low


def project_kernel(x_hbm, g_hbm, px_hbm, pg_hbm, keep_ref, send_ref, xb, gb, pxb, pgb, wx_ref, wg_ref, sx, sg, sp):
    y, zl, c = (lax.axis_index(a) for a in HID)
    starts = [sum(SIZES[:i]) for i in range(len(SIZES))]

    def fetch(i):
        rows = pl.ds(starts[i], SIZES[i])
        copies = (
            pltpu.make_async_copy(x_hbm.at[rows], xb.at[rows], sx.at[i]),
            pltpu.make_async_copy(g_hbm.at[rows], gb.at[rows], sg.at[i]),
        )
        for copy in copies:
            copy.start()
        return copies

    weights = [pltpu.make_async_copy(px_hbm, pxb, sp.at[0])] + [
        pltpu.make_async_copy(pg_hbm.at[:, k * LANES : (k + 1) * LANES], pgb.at[k], sp.at[1 + k]) for k in range(2)
    ]
    for copy in weights:
        copy.start()
    live = {i: fetch(i) for i in range(2)}
    for copy in weights:
        copy.wait()
    xh, xl = split(pxb[...].T)
    zx = jnp.zeros_like(xh)
    wx_ref[:, :LANES] = jnp.concatenate([zx, xh], axis=1)
    wx_ref[:, LANES:] = jnp.concatenate([zx, xl], axis=1)
    order = [pl.ds(parity, RANK // 2, stride=2) for parity in range(2)]
    halves = [jnp.concatenate([pgb[k, rows, :] for rows in order], axis=0).T for k in range(2)]
    gh, gl = split(jnp.concatenate(halves, axis=0))
    zg = jnp.zeros_like(gh)
    wg_ref[:, :LANES] = jnp.concatenate([gh, zg], axis=1)
    wg_ref[:, LANES:] = jnp.concatenate([gl, zg], axis=1)

    dot = functools.partial(jnp.dot, preferred_element_type=F32)
    for i in range(len(SIZES)):
        if i + 2 < len(SIZES):
            live[i + 2] = fetch(i + 2)
        for copy in live[i]:
            copy.wait()
        rows = slice(starts[i], starts[i] + SIZES[i])
        xh, xl = split(xb[rows])
        gh, gl = split(gb[rows])
        acc = dot(xh, wx_ref[...]) + dot(gh, wg_ref[...])
        low = dot(xl, wx_ref[:, :LANES]) + dot(gl, wg_ref[:, :LANES])
        total = acc[:, :LANES] + (acc[:, LANES:] + low)
        for half in range(SIZES[i] // HALF):
            block = starts[i] // HALF + half
            seq, side = block // 2, block % 2

            def put(ref):
                for q in range(4):
                    at = pl.multiple_of((q ^ zl) * CHUNK, CHUNK)
                    first = half * HALF + q * CHUNK
                    ref[seq ^ y, pl.ds(at, CHUNK), :] = total[first : first + CHUNK]

            @pl.when(c == side)
            def _():
                put(keep_ref)

            @pl.when(c != side)
            def _():
                put(send_ref)


def project(activations, out_grads, input_proj, output_proj):
    rows, d_in = activations.shape
    d_out = out_grads.shape[1]
    shape = jax.ShapeDtypeStruct((E_DEV, HALF, LANES), F32)
    operands = [activations, out_grads, input_proj.T, output_proj.T]
    return pl.pallas_call(
        project_kernel,
        out_shape=(shape, shape),
        in_specs=[pl.BlockSpec(memory_space=pltpu.HBM)] * 4,
        out_specs=[pl.BlockSpec(memory_space=pltpu.VMEM)] * 2,
        scratch_shapes=[
            pltpu.VMEM((rows, d_in), F32),
            pltpu.VMEM((rows, d_out), F32),
            pltpu.VMEM((RANK, d_in), F32),
            pltpu.VMEM((2, RANK, LANES), F32),
            pltpu.VMEM((d_in, 2 * LANES), BF16),
            pltpu.VMEM((d_out, 2 * LANES), BF16),
            pltpu.SemaphoreType.DMA((len(SIZES),)),
            pltpu.SemaphoreType.DMA((len(SIZES),)),
            pltpu.SemaphoreType.DMA((3,)),
        ],
        compiler_params=pltpu.CompilerParams(vmem_limit_bytes=14 << 20),
        cost_estimate=pl.CostEstimate(flops=3 << 30, bytes_accessed=10 << 20, transcendentals=0),
        name="project",
    )(*[pltpu.with_memory_space_constraint(v, pltpu.HBM) for v in operands])


def outer_kernel(a_ref, b_ref, c_ref, d_ref, out_ref):
    rows = a_ref[...] + b_ref[...] + c_ref[...] + d_ref[...]
    high, low = split(rows.T[:RANK])
    xh, xl = split(rows)
    dot = functools.partial(jnp.dot, preferred_element_type=F32)
    acc = dot(high, xh) + dot(high, xl) + dot(low, xh)
    right = acc[:, RANK:]
    out_ref[...] = jnp.concatenate([right[: RANK // 2], right[RANK // 2 :]], axis=1)


def outer(pieces):
    return pl.pallas_call(
        outer_kernel,
        out_shape=jax.ShapeDtypeStruct((FEAT // LANES, LANES), F32),
        compiler_params=pltpu.CompilerParams(vmem_limit_bytes=4 << 20),
        name="outer",
    )(*pieces)


def score_kernel(grads_ref, *refs):
    zh, x, y = (lax.axis_index(a) for a in ("zh", "x", "y"))
    near, one, three, two_a, two_b, out_ref, all_ref = refs
    pieces = ((near, one, three), (two_a, two_b))
    tiles = FEAT // LANES
    for e, bits in enumerate((0, 1, 3, 2)):
        all_ref[pl.ds(pl.multiple_of((y ^ bits) * tiles, tiles), tiles), :] = grads_ref[e]
    acc = jnp.zeros((2 * E_DEV, 2 * LANES), F32)
    for at, dx in enumerate((0, 1, 3, 2)):
        for dz in range(2):
            base = ((zh ^ dz) * 4 + (x ^ dx)) * 4
            left = jnp.concatenate(
                [all_ref[pl.ds(base + t, E_DEV, stride=tiles), :] for t in range(4)], axis=1
            )
            lh, ll = split(left)
            lhs = jnp.concatenate([lh.astype(F32), ll.astype(F32)], axis=0).astype(BF16)
            qh, ql = split(pieces[0][at][dz] if at < 3 else pieces[1][dz][...])
            acc = acc + jnp.dot(lhs, jnp.concatenate([qh, ql], axis=1), preferred_element_type=F32)
    out_ref[...] = acc[:E_DEV, :LANES] + (acc[:E_DEV, LANES:] + acc[E_DEV:, :LANES])


def score(grads, blocks):
    vmem = pl.BlockSpec(memory_space=pltpu.VMEM)
    return pl.pallas_call(
        score_kernel,
        out_shape=jax.ShapeDtypeStruct((E_DEV, LANES), F32),
        in_specs=[vmem] * 6,
        out_specs=vmem,
        scratch_shapes=[pltpu.VMEM((FEAT // LANES * E_DEV, LANES), F32)],
        compiler_params=pltpu.CompilerParams(vmem_limit_bytes=6 << 20),
        name="score",
    )(grads, *blocks)


def swap(value, axis, size, bits):
    return lax.ppermute(value, axis, [(i, i ^ bits) for i in range(size)])


def on_device(activations, out_grads, input_proj, output_proj, query_grads):
    keep, send = project(activations, out_grads, input_proj, output_proj)
    query, send = lax.optimization_barrier((query_grads, send))
    far = swap(query, "zh", 2, 1)
    part = keep + swap(send, "c", 2, 1)
    near = jnp.stack([query, far])
    one, three = swap(near, "x", 4, 1), swap(near, "x", 4, 3)
    rows = part[0] + sum(swap(part[k], "y", 4, k) for k in (1, 3, 2))
    pieces = [rows[m * CHUNK : (m + 1) * CHUNK] for m in range(4)]
    pieces = pieces[:1] + [swap(pieces[m], "zl", 4, m) for m in (1, 2, 3)]
    grads = outer(pieces)
    two = [swap(three[0], "x", 4, 1), swap(one[1], "x", 4, 3)]
    grads = grads + swap(grads, "c", 2, 1)
    grads = grads + (swap(grads, "zl", 4, 1) + swap(grads, "zl", 4, 2) + swap(grads, "zl", 4, 3))
    both = jnp.stack([grads] + [swap(grads, "y", 4, k) for k in (1, 3, 2)])
    return score(both, [near, one, three] + two)


def solution(mesh):
    fine = Mesh(mesh.devices.reshape(2, 4, 4, 4, 2), EX + HID)
    placed = (P(EX, HID), P(EX, HID), P(HID, None), P(HID, None), P(EX, HID))
    return jax.shard_map(on_device, mesh=fine, in_specs=placed, out_specs=P(EX, HID), check_vma=False)
```

```python
import functools

import jax
import jax.numpy as jnp
from jax import lax
from jax.experimental import pallas as pl
from jax.experimental.pallas import tpu as pltpu
from jax.sharding import Mesh, PartitionSpec as P

RANK = 64
SEQ = 512
E_DEV = 4
FEAT = 4096
LANES = 128
HALF = SEQ // 2
CHUNK = HALF // 4
SIZES = (512, 512, 512, 512)
HID = ("y", "zl", "c")
EX = ("zh", "x")
F32 = jnp.float32
BF16 = jnp.bfloat16


def split(value):
    high = value.astype(BF16)
    low = (value - high.astype(F32)).astype(BF16)
    return high, low


def project_kernel(x_hbm, g_hbm, px_hbm, pg_hbm, keep_ref, send_ref, xb, gb, pxb, pgb, wx_ref, wg_ref, sx, sg, sp):
    y, zl, c = (lax.axis_index(a) for a in HID)
    starts = [sum(SIZES[:i]) for i in range(len(SIZES))]

    def fetch(i):
        rows = pl.ds(starts[i], SIZES[i])
        copies = (
            pltpu.make_async_copy(x_hbm.at[rows], xb.at[rows], sx.at[i]),
            pltpu.make_async_copy(g_hbm.at[rows], gb.at[rows], sg.at[i]),
        )
        for copy in copies:
            copy.start()
        return copies

    weights = [pltpu.make_async_copy(px_hbm, pxb, sp.at[0])] + [
        pltpu.make_async_copy(pg_hbm.at[:, k * LANES : (k + 1) * LANES], pgb.at[k], sp.at[1 + k]) for k in range(2)
    ]
    for copy in weights:
        copy.start()
    live = {i: fetch(i) for i in range(2)}
    for copy in weights:
        copy.wait()
    xh, xl = split(pxb[...].T)
    zx = jnp.zeros_like(xh)
    wx_ref[:, :LANES] = jnp.concatenate([zx, xh], axis=1)
    wx_ref[:, LANES:] = jnp.concatenate([zx, xl], axis=1)
    order = [pl.ds(parity, RANK // 2, stride=2) for parity in range(2)]
    halves = [jnp.concatenate([pgb[k, rows, :] for rows in order], axis=0).T for k in range(2)]
    gh, gl = split(jnp.concatenate(halves, axis=0))
    zg = jnp.zeros_like(gh)
    wg_ref[:, :LANES] = jnp.concatenate([gh, zg], axis=1)
    wg_ref[:, LANES:] = jnp.concatenate([gl, zg], axis=1)

    dot = functools.partial(jnp.dot, preferred_element_type=F32)
    for i in range(len(SIZES)):
        if i + 2 < len(SIZES):
            live[i + 2] = fetch(i + 2)
        for copy in live[i]:
            copy.wait()
        rows = slice(starts[i], starts[i] + SIZES[i])
        xh, xl = split(xb[rows])
        gh, gl = split(gb[rows])
        acc = dot(xh, wx_ref[...]) + dot(gh, wg_ref[...])
        low = dot(xl, wx_ref[:, :LANES]) + dot(gl, wg_ref[:, :LANES])
        total = acc[:, :LANES] + (acc[:, LANES:] + low)
        for half in range(SIZES[i] // HALF):
            block = starts[i] // HALF + half
            seq, side = block // 2, block % 2

            def put(ref):
                for q in range(4):
                    at = pl.multiple_of((q ^ zl) * CHUNK, CHUNK)
                    first = half * HALF + q * CHUNK
                    ref[seq ^ y, pl.ds(at, CHUNK), :] = total[first : first + CHUNK]

            @pl.when(c == side)
            def _():
                put(keep_ref)

            @pl.when(c != side)
            def _():
                put(send_ref)


def project(activations, out_grads, input_proj, output_proj):
    rows, d_in = activations.shape
    d_out = out_grads.shape[1]
    shape = jax.ShapeDtypeStruct((E_DEV, HALF, LANES), F32)
    operands = [activations, out_grads, input_proj.T, output_proj.T]
    return pl.pallas_call(
        project_kernel,
        out_shape=(shape, shape),
        in_specs=[pl.BlockSpec(memory_space=pltpu.HBM)] * 4,
        out_specs=[pl.BlockSpec(memory_space=pltpu.VMEM)] * 2,
        scratch_shapes=[
            pltpu.VMEM((rows, d_in), F32),
            pltpu.VMEM((rows, d_out), F32),
            pltpu.VMEM((RANK, d_in), F32),
            pltpu.VMEM((2, RANK, LANES), F32),
            pltpu.VMEM((d_in, 2 * LANES), BF16),
            pltpu.VMEM((d_out, 2 * LANES), BF16),
            pltpu.SemaphoreType.DMA((len(SIZES),)),
            pltpu.SemaphoreType.DMA((len(SIZES),)),
            pltpu.SemaphoreType.DMA((3,)),
        ],
        compiler_params=pltpu.CompilerParams(vmem_limit_bytes=14 << 20),
        cost_estimate=pl.CostEstimate(flops=3 << 30, bytes_accessed=10 << 20, transcendentals=0),
        name="project",
    )(*[pltpu.with_memory_space_constraint(v, pltpu.HBM) for v in operands])


def outer_kernel(a_ref, b_ref, c_ref, d_ref, out_ref):
    rows = a_ref[...] + b_ref[...] + c_ref[...] + d_ref[...]
    high, low = split(rows.T[:RANK])
    xh, xl = split(rows)
    dot = functools.partial(jnp.dot, preferred_element_type=F32)
    acc = dot(high, xh) + dot(high, xl) + dot(low, xh)
    right = acc[:, RANK:]
    out_ref[...] = jnp.concatenate([right[: RANK // 2], right[RANK // 2 :]], axis=1)


def outer(pieces):
    return pl.pallas_call(
        outer_kernel,
        out_shape=jax.ShapeDtypeStruct((FEAT // LANES, LANES), F32),
        compiler_params=pltpu.CompilerParams(vmem_limit_bytes=4 << 20),
        name="outer",
    )(*pieces)


def score_kernel(grads_ref, *refs):
    zh, x, y = (lax.axis_index(a) for a in ("zh", "x", "y"))
    near, one, three, two_a, two_b, out_ref, all_ref = refs
    pieces = ((near, one, three), (two_a, two_b))
    tiles = FEAT // LANES
    for e, bits in enumerate((0, 2, 3, 1)):
        all_ref[pl.ds(pl.multiple_of((y ^ bits) * tiles, tiles), tiles), :] = grads_ref[e]
    acc = jnp.zeros((2 * E_DEV, 2 * LANES), F32)
    for at, dx in enumerate((0, 1, 3, 2)):
        for dz in range(2):
            base = ((zh ^ dz) * 4 + (x ^ dx)) * 4
            left = jnp.concatenate(
                [all_ref[pl.ds(base + t, E_DEV, stride=tiles), :] for t in range(4)], axis=1
            )
            lh, ll = split(left)
            lhs = jnp.concatenate([lh.astype(F32), ll.astype(F32)], axis=0).astype(BF16)
            qh, ql = split(pieces[0][at][dz] if at < 3 else pieces[1][dz][...])
            acc = acc + jnp.dot(lhs, jnp.concatenate([qh, ql], axis=1), preferred_element_type=F32)
    out_ref[...] = acc[:E_DEV, :LANES] + (acc[:E_DEV, LANES:] + acc[E_DEV:, :LANES])


def score(grads, blocks):
    vmem = pl.BlockSpec(memory_space=pltpu.VMEM)
    return pl.pallas_call(
        score_kernel,
        out_shape=jax.ShapeDtypeStruct((E_DEV, LANES), F32),
        in_specs=[vmem] * 6,
        out_specs=vmem,
        scratch_shapes=[pltpu.VMEM((FEAT // LANES * E_DEV, LANES), F32)],
        compiler_params=pltpu.CompilerParams(vmem_limit_bytes=6 << 20),
        name="score",
    )(grads, *blocks)


def swap(value, axis, size, bits):
    return lax.ppermute(value, axis, [(i, i ^ bits) for i in range(size)])


def on_device(activations, out_grads, input_proj, output_proj, query_grads):
    keep, send = project(activations, out_grads, input_proj, output_proj)
    query, send = lax.optimization_barrier((query_grads, send))
    far = swap(query, "zh", 2, 1)
    part = keep + swap(send, "c", 2, 1)
    near = jnp.stack([query, far])
    one, three = swap(near, "x", 4, 1), swap(near, "x", 4, 3)
    rows = part[0] + sum(swap(part[k], "y", 4, k) for k in (1, 3, 2))
    pieces = [rows[m * CHUNK : (m + 1) * CHUNK] for m in range(4)]
    pieces = pieces[:1] + [swap(pieces[m], "zl", 4, m) for m in (3, 2, 1)]
    grads = outer(pieces)
    two = [swap(three[0], "x", 4, 1), swap(one[1], "x", 4, 3)]
    grads = grads + swap(grads, "c", 2, 1)
    grads = grads + (swap(grads, "zl", 4, 3) + swap(grads, "zl", 4, 2) + swap(grads, "zl", 4, 1))
    both = jnp.stack([grads] + [swap(grads, "y", 4, k) for k in (2, 3, 1)])
    return score(both, [near, one, three] + two)


def solution(mesh):
    fine = Mesh(mesh.devices.reshape(2, 4, 4, 4, 2), EX + HID)
    placed = (P(EX, HID), P(EX, HID), P(HID, None), P(HID, None), P(EX, HID))
    return jax.shard_map(on_device, mesh=fine, in_specs=placed, out_specs=P(EX, HID), check_vma=False)
```

```python
import functools

import jax
import jax.numpy as jnp
from jax import lax
from jax.experimental import pallas as pl
from jax.experimental.pallas import tpu as pltpu
from jax.sharding import Mesh, PartitionSpec as P

RANK = 64
SEQ = 512
E_DEV = 4
FEAT = 4096
LANES = 128
HALF = SEQ // 2
CHUNK = HALF // 4
SIZES = (512, 512, 512, 512)
HID = ("y", "zl", "c")
EX = ("zh", "x")
F32 = jnp.float32
BF16 = jnp.bfloat16


def split(value):
    high = value.astype(BF16)
    low = (value - high.astype(F32)).astype(BF16)
    return high, low


def project_kernel(x_hbm, g_hbm, px_hbm, pg_hbm, keep_ref, send_ref, xb, gb, pxb, pgb, wx_ref, wg_ref, sx, sg, sp):
    y, zl, c = (lax.axis_index(a) for a in HID)
    starts = [sum(SIZES[:i]) for i in range(len(SIZES))]

    def fetch(i):
        rows = pl.ds(starts[i], SIZES[i])
        copies = (
            pltpu.make_async_copy(x_hbm.at[rows], xb.at[rows], sx.at[i]),
            pltpu.make_async_copy(g_hbm.at[rows], gb.at[rows], sg.at[i]),
        )
        for copy in copies:
            copy.start()
        return copies

    weights = [pltpu.make_async_copy(px_hbm, pxb, sp.at[0])] + [
        pltpu.make_async_copy(pg_hbm.at[:, k * LANES : (k + 1) * LANES], pgb.at[k], sp.at[1 + k]) for k in range(2)
    ]
    for copy in weights:
        copy.start()
    live = {i: fetch(i) for i in range(2)}
    for copy in weights:
        copy.wait()
    xh, xl = split(pxb[...].T)
    zx = jnp.zeros_like(xh)
    wx_ref[:, :LANES] = jnp.concatenate([zx, xh], axis=1)
    wx_ref[:, LANES:] = jnp.concatenate([zx, xl], axis=1)
    order = [pl.ds(parity, RANK // 2, stride=2) for parity in range(2)]
    halves = [jnp.concatenate([pgb[k, rows, :] for rows in order], axis=0).T for k in range(2)]
    gh, gl = split(jnp.concatenate(halves, axis=0))
    zg = jnp.zeros_like(gh)
    wg_ref[:, :LANES] = jnp.concatenate([gh, zg], axis=1)
    wg_ref[:, LANES:] = jnp.concatenate([gl, zg], axis=1)

    dot = functools.partial(jnp.dot, preferred_element_type=F32)
    for i in range(len(SIZES)):
        if i + 2 < len(SIZES):
            live[i + 2] = fetch(i + 2)
        for copy in live[i]:
            copy.wait()
        rows = slice(starts[i], starts[i] + SIZES[i])
        xh, xl = split(xb[rows])
        gh, gl = split(gb[rows])
        acc = dot(xh, wx_ref[...]) + dot(gh, wg_ref[...])
        low = dot(xl, wx_ref[:, :LANES]) + dot(gl, wg_ref[:, :LANES])
        total = acc[:, :LANES] + (acc[:, LANES:] + low)
        for half in range(SIZES[i] // HALF):
            block = starts[i] // HALF + half
            seq, side = block // 2, block % 2

            def put(ref):
                for q in range(4):
                    at = pl.multiple_of((q ^ zl) * CHUNK, CHUNK)
                    first = half * HALF + q * CHUNK
                    ref[seq ^ y, pl.ds(at, CHUNK), :] = total[first : first + CHUNK]

            @pl.when(c == side)
            def _():
                put(keep_ref)

            @pl.when(c != side)
            def _():
                put(send_ref)


def project(activations, out_grads, input_proj, output_proj):
    rows, d_in = activations.shape
    d_out = out_grads.shape[1]
    shape = jax.ShapeDtypeStruct((E_DEV, HALF, LANES), F32)
    operands = [activations, out_grads, input_proj.T, output_proj.T]
    return pl.pallas_call(
        project_kernel,
        out_shape=(shape, shape),
        in_specs=[pl.BlockSpec(memory_space=pltpu.HBM)] * 4,
        out_specs=[pl.BlockSpec(memory_space=pltpu.VMEM)] * 2,
        scratch_shapes=[
            pltpu.VMEM((rows, d_in), F32),
            pltpu.VMEM((rows, d_out), F32),
            pltpu.VMEM((RANK, d_in), F32),
            pltpu.VMEM((2, RANK, LANES), F32),
            pltpu.VMEM((d_in, 2 * LANES), BF16),
            pltpu.VMEM((d_out, 2 * LANES), BF16),
            pltpu.SemaphoreType.DMA((len(SIZES),)),
            pltpu.SemaphoreType.DMA((len(SIZES),)),
            pltpu.SemaphoreType.DMA((3,)),
        ],
        compiler_params=pltpu.CompilerParams(vmem_limit_bytes=14 << 20),
        cost_estimate=pl.CostEstimate(flops=3 << 30, bytes_accessed=10 << 20, transcendentals=0),
        name="project",
    )(*[pltpu.with_memory_space_constraint(v, pltpu.HBM) for v in operands])


def outer_kernel(a_ref, b_ref, c_ref, d_ref, out_ref):
    rows = a_ref[...] + b_ref[...] + c_ref[...] + d_ref[...]
    high, low = split(rows.T[:RANK])
    xh, xl = split(rows)
    dot = functools.partial(jnp.dot, preferred_element_type=F32)
    acc = dot(high, xh) + dot(high, xl) + dot(low, xh)
    right = acc[:, RANK:]
    out_ref[...] = jnp.concatenate([right[: RANK // 2], right[RANK // 2 :]], axis=1)


def outer(pieces):
    return pl.pallas_call(
        outer_kernel,
        out_shape=jax.ShapeDtypeStruct((FEAT // LANES, LANES), F32),
        compiler_params=pltpu.CompilerParams(vmem_limit_bytes=4 << 20),
        name="outer",
    )(*pieces)


def score_kernel(grads_ref, *refs):
    zh, x, y = (lax.axis_index(a) for a in ("zh", "x", "y"))
    near, one, three, two_a, two_b, out_ref, all_ref = refs
    pieces = ((near, one, three), (two_a, two_b))
    tiles = FEAT // LANES
    for e, bits in enumerate((0, 2, 3, 1)):
        all_ref[pl.ds(pl.multiple_of((y ^ bits) * tiles, tiles), tiles), :] = grads_ref[e]
    acc = jnp.zeros((2 * E_DEV, 2 * LANES), F32)
    for at, dx in enumerate((0, 1, 3, 2)):
        for dz in range(2):
            base = ((zh ^ dz) * 4 + (x ^ dx)) * 4
            left = jnp.concatenate(
                [all_ref[pl.ds(base + t, E_DEV, stride=tiles), :] for t in range(4)], axis=1
            )
            lh, ll = split(left)
            lhs = jnp.concatenate([lh.astype(F32), ll.astype(F32)], axis=0).astype(BF16)
            qh, ql = split(pieces[0][at][dz] if at < 3 else pieces[1][dz][...])
            acc = acc + jnp.dot(lhs, jnp.concatenate([qh, ql], axis=1), preferred_element_type=F32)
    out_ref[...] = acc[:E_DEV, :LANES] + (acc[:E_DEV, LANES:] + acc[E_DEV:, :LANES])


def score(grads, blocks):
    vmem = pl.BlockSpec(memory_space=pltpu.VMEM)
    return pl.pallas_call(
        score_kernel,
        out_shape=jax.ShapeDtypeStruct((E_DEV, LANES), F32),
        in_specs=[vmem] * 6,
        out_specs=vmem,
        scratch_shapes=[pltpu.VMEM((FEAT // LANES * E_DEV, LANES), F32)],
        compiler_params=pltpu.CompilerParams(vmem_limit_bytes=6 << 20),
        name="score",
    )(grads, *blocks)


def swap(value, axis, size, bits):
    return lax.ppermute(value, axis, [(i, i ^ bits) for i in range(size)])


def on_device(activations, out_grads, input_proj, output_proj, query_grads):
    keep, send = project(activations, out_grads, input_proj, output_proj)
    query, send = lax.optimization_barrier((query_grads, send))
    far = swap(query, "zh", 2, 1)
    part = keep + swap(send, "c", 2, 1)
    near = jnp.stack([query, far])
    one, three = swap(near, "x", 4, 1), swap(near, "x", 4, 3)
    rows = part[0] + sum(swap(part[k], "y", 4, k) for k in (1, 3, 2))
    pieces = [rows[m * CHUNK : (m + 1) * CHUNK] for m in range(4)]
    pieces = pieces[:1] + [swap(pieces[m], "zl", 4, m) for m in (3, 2, 1)]
    grads = outer(pieces)
    two = [swap(three[0], "x", 4, 1), swap(one[1], "x", 4, 3)]
    grads = grads + swap(grads, "c", 2, 1)
    grads = grads + (swap(grads, "zl", 4, 2) + swap(grads, "zl", 4, 1) + swap(grads, "zl", 4, 3))
    both = jnp.stack([grads] + [swap(grads, "y", 4, k) for k in (2, 3, 1)])
    return score(both, [near, one, three] + two)


def solution(mesh):
    fine = Mesh(mesh.devices.reshape(2, 4, 4, 4, 2), EX + HID)
    placed = (P(EX, HID), P(EX, HID), P(HID, None), P(HID, None), P(EX, HID))
    return jax.shard_map(on_device, mesh=fine, in_specs=placed, out_specs=P(EX, HID), check_vma=False)
```
